32 devices in a mesh: grp: 2 (over y), gx: 8 (over z, x), rep: 2 (over core).
Axes of the slice: x: 2, y: 2, z: 4, core: 2. Of those that a mesh axis runs over, the one named last changes fastest.
Arguments:
- fields: bfloat16 [4, 128, 32, 128, 128], P(('grp', 'rep'), 'gx'), parts along dimension 0, may hold values from -6 to 6
- targets: bfloat16 [4, 128, 3, 128, 128], P(('grp', 'rep'), 'gx'), parts along dimension 0, may hold values from -3 to 3
- multipliers: int32 [4, 128, 128, 128], P(('grp', 'rep'), 'gx'), parts along dimension 0, may hold values from -256 to 256
- local_weight: bfloat16 [32, 32], replicated, may hold values from -1 to 1
- proj_weight: bfloat16 [32, 3], replicated, may hold values from -1 to 1
- spectral_weight: bfloat16 [16, 256, 2, 32, 32], P('rep', 'gx'), may hold values from -9 to 9
Outputs:
- new_multipliers: float32 [4, 128, 128, 128], P(('grp', 'rep'), 'gx'), parts along dimension 0
- grad_spectral: float32 [32, 256, 2, 32, 32], P(('grp', 'rep'), 'gx'), parts along dimension 0
- grad_local: float32 [64, 32], P('grp'), parts along dimension 0
- grad_proj: float32 [64, 3], P('grp'), parts along dimension 0
- loss: float32 [2], P('grp'), parts along dimension 0
The draws below stay inside these ranges and needn't reach their ends.
There are 2 independent parts, one for each index of `grp`. The reference program is written for one: setup_inputs(seed, part) draws one part's arguments, and reference() takes and returns one part's arrays. A program takes and returns all parts, laid end to end along the dimension named above; an argument that names none is the same for every part. Nothing has to cross between parts.
All inputs are finite; a program needn't handle non-finite values.
Results may differ from the reference program's by a relative error of at most 0.0005.
The reference program's roundings to bfloat16 on the way count: a program that leaves them out, or rounds other values in their place, can miss the bound.
Values may be sent and summed in bfloat16 or wider, within the bound.
A program may use at most 256 MiB of HBM per device.

```python
import math
import jax
import jax.numpy as jnp
from jax import lax

C = 32
NX = 128
NY = 128
NZ = 128
MX = 16
MY = 16
MZ = 16
BATCH = 2
PAIRS = 256


def set_ends(result, own_key, low, top_value):
    longest = result.shape.index(max(result.shape))
    spots = []
    for shift in (0, 1):
        where = [jax.random.randint(jax.random.fold_in(own_key, axis), (), 0, length) for axis, length in enumerate(result.shape)]
        where[longest] = (where[longest] + shift) % result.shape[longest]
        spots.append(tuple(where))
    return result.at[spots[0]].set(low).at[spots[1]].set(top_value)


def levels(own_key, extent, shards, smallest, high):
    level, own = 1.0, jax.random.fold_in(own_key, 6)
    for dim, shards_of in shards:
        steps = jnp.exp(jax.random.uniform(jax.random.fold_in(own, dim), (shards_of,), jnp.float32, smallest / len(shards), high / len(shards)))
        level = level * jnp.repeat(steps, extent[dim] // shards_of).reshape([-1 if axis == dim else 1 for axis in range(len(extent))])
    return level


def centred(stream_key, shape, deviation, reach, split=(), held_as=jnp.bfloat16):
    level = levels(stream_key, shape, split, -0.22, 0.18) if split else 1.0
    drawn = jax.random.normal(stream_key, shape, jnp.float32) * deviation * level
    return jnp.minimum(jnp.maximum(drawn, -reach), reach).astype(held_as)


def setup_inputs(seed: int = 0, part: int = 0) -> dict:
    streams_of = jax.random.split(jax.random.key(seed), 7)
    part_keys = jax.random.split(jax.random.fold_in(streams_of[6], part), 7)
    return {
        "fields": centred(part_keys[0], (BATCH, NX, C, NY, NZ), 1.0, 6.0, ((0, 2), (1, 8))),
        "targets": centred(part_keys[1], (BATCH, NX, 3, NY, NZ), 0.5, 3.0, ((0, 2), (1, 8))),
        "multipliers": set_ends(jax.random.randint(part_keys[2], (BATCH, NX, NY, NZ), -256, 257), jax.random.fold_in(part_keys[2], 1), -256, 256).astype(jnp.int32),
        "local_weight": centred(streams_of[3], (C, C), C ** -0.5, 1.0),
        "proj_weight": centred(streams_of[4], (C, 3), C ** -0.5, 1.0),
        "spectral_weight": centred(streams_of[5], (MX, PAIRS, 2, C, C), 1.5, 9.0, ((0, 2), (1, 8))),
    }


penalty_weight = 0.5
precise = lax.Precision.HIGHEST

def widen(values):
    return lax.optimization_barrier(values).astype(jnp.float32)

def mode_numbers(count):
    position = jnp.arange(count, dtype=jnp.int32)
    return jnp.where(position < count // 2, position, position - count)

def fourier_tables(length, count):
    cells = jnp.arange(length, dtype=jnp.int32)
    phase = jnp.mod(cells[:, None] * mode_numbers(count)[None, :], length)
    angle = phase.astype(jnp.float32) * (2.0 * math.pi / length)
    return (jnp.cos(angle), jnp.sin(angle))

def to_last(values, table):
    return jnp.einsum('...kz,zm->...km', values, table, precision=precise)

def from_last(values, table):
    return jnp.einsum('...km,zm->...kz', values, table, precision=precise)

def forward_plane(field):
    cos_y, sin_y = fourier_tables(NY, MY)
    lookup_table_y = jnp.stack([cos_y, -sin_y], axis=1).astype(jnp.bfloat16)
    partial_value = jnp.einsum('...cyz,yrk->...crkz', widen(field), widen(lookup_table_y), precision=precise)
    cos_z, sin_z = fourier_tables(NZ, MZ)
    real_part = partial_value[..., 0, :, :]
    imag_part = partial_value[..., 1, :, :]
    spec_re = to_last(real_part, cos_z) + to_last(imag_part, sin_z)
    spec_im = to_last(imag_part, cos_z) - to_last(real_part, sin_z)
    stacked = jnp.stack([spec_re, spec_im], axis=-3)
    return stacked.reshape(stacked.shape[:-2] + (MY * MZ,))

def forward_x(slab, normalize_scale):
    cos_x, sin_x = fourier_tables(NX, MX)
    real_part = slab[:, :, :, 0]
    imag_part = slab[:, :, :, 1]
    spec_re = jnp.einsum('bxcp,xm->bmcp', real_part, cos_x, precision=precise) + jnp.einsum('bxcp,xm->bmcp', imag_part, sin_x, precision=precise)
    spec_im = jnp.einsum('bxcp,xm->bmcp', imag_part, cos_x, precision=precise) - jnp.einsum('bxcp,xm->bmcp', real_part, sin_x, precision=precise)
    return jnp.stack([spec_re, spec_im], axis=3) * normalize_scale

def multiply(weights, spectrum):
    w_re = weights[:, :, 0]
    w_im = weights[:, :, 1]
    s_re = spectrum[:, :, :, 0]
    s_im = spectrum[:, :, :, 1]
    t_re = jnp.einsum('mpoc,bmcp->bmop', w_re, s_re, precision=precise) - jnp.einsum('mpoc,bmcp->bmop', w_im, s_im, precision=precise)
    t_im = jnp.einsum('mpoc,bmcp->bmop', w_re, s_im, precision=precise) + jnp.einsum('mpoc,bmcp->bmop', w_im, s_re, precision=precise)
    return jnp.stack([t_re, t_im], axis=3)

def inverse_x(modes):
    cos_x, sin_x = fourier_tables(NX, MX)
    t_re = modes[:, :, :, 0]
    t_im = modes[:, :, :, 1]
    out_re = jnp.einsum('bmop,xm->bxop', t_re, cos_x, precision=precise) - jnp.einsum('bmop,xm->bxop', t_im, sin_x, precision=precise)
    output_imaginary = jnp.einsum('bmop,xm->bxop', t_im, cos_x, precision=precise) + jnp.einsum('bmop,xm->bxop', t_re, sin_x, precision=precise)
    return jnp.stack([out_re, output_imaginary], axis=3)

def inverse_plane(wave, normalize_scale):
    reshaped_array = wave.reshape(wave.shape[:-1] + (MY, MZ))
    w_re = reshaped_array[..., 0, :, :]
    w_im = reshaped_array[..., 1, :, :]
    cos_z, sin_z = fourier_tables(NZ, MZ)
    q_re = from_last(w_re, cos_z) - from_last(w_im, sin_z)
    q_im = from_last(w_im, cos_z) + from_last(w_re, sin_z)
    rounded = jnp.stack([q_re, q_im], axis=-3).astype(jnp.bfloat16)
    cos_y, sin_y = fourier_tables(NY, MY)
    lookup_table_y = jnp.stack([cos_y.T, -sin_y.T]).astype(jnp.bfloat16)
    return jnp.einsum('...orkz,rky->...oyz', widen(rounded), widen(lookup_table_y), precision=precise) * normalize_scale

def mode_grads(grads, spectrum):
    g_re = grads[:, :, :, 0]
    g_im = grads[:, :, :, 1]
    s_re = spectrum[:, :, :, 0]
    s_im = spectrum[:, :, :, 1]
    d_re = jnp.einsum('bmop,bmcp->mpoc', g_re, s_re, precision=precise) + jnp.einsum('bmop,bmcp->mpoc', g_im, s_im, precision=precise)
    d_im = jnp.einsum('bmop,bmcp->mpoc', g_im, s_re, precision=precise) - jnp.einsum('bmop,bmcp->mpoc', g_re, s_im, precision=precise)
    return jnp.stack([d_re, d_im], axis=2)

def central(values, axis):
    return (jnp.roll(values, -1, axis) - jnp.roll(values, 1, axis)) * 0.5

def reference(fields, targets, multipliers, local_weight, proj_weight, spectral_weight):
    normalize_scale = 1.0 / math.sqrt(NX * NY * NZ)
    weights = widen(spectral_weight)
    w_local = widen(local_weight)
    w_proj = widen(proj_weight)

    def plane_forward(plane, wave):
        preact = jnp.einsum('cyz,co->oyz', widen(plane), w_local, precision=precise) + inverse_plane(wave, normalize_scale)
        hidden = jax.nn.gelu(preact).astype(jnp.bfloat16)
        velocity = jnp.einsum('oyz,oj->jyz', widen(hidden), w_proj, precision=precise)
        return (preact, hidden, velocity)

    def plane_backward(sums, inputs):
        plane, wave, grad_vel = inputs
        preact, hidden, unused = plane_forward(plane, wave)
        grad_hidden = jnp.einsum('jyz,oj->oyz', widen(grad_vel), w_proj, precision=precise)
        grad_pre = jax.vjp(jax.nn.gelu, preact)[1](grad_hidden)[0].astype(jnp.bfloat16)
        grad_w = sums[0] + jnp.einsum('cyz,oyz->co', widen(plane), widen(grad_pre), precision=precise)
        grad_q = sums[1] + jnp.einsum('oyz,jyz->oj', widen(hidden), widen(grad_vel), precision=precise)
        return ((grad_w, grad_q), forward_plane(grad_pre))

    def single_example(total_sums, inputs):
        field, target, multiplier = inputs
        slab = lax.map(forward_plane, field)
        spectrum = forward_x(slab[None], normalize_scale)
        back = inverse_x(multiply(weights, spectrum))[0]
        velocity = lax.map(lambda pair: plane_forward(pair[0], pair[1])[2], (field, back))
        divergence = central(velocity[:, 0], 0) + central(velocity[:, 1], 1) + central(velocity[:, 2], 2)
        lam = multiplier.astype(jnp.float32) / 64.0
        penalty = lam + penalty_weight * divergence
        misfit = velocity - widen(target)
        loss_sum = jnp.sum(misfit * misfit) + jnp.sum(lam * divergence) + 0.5 * penalty_weight * jnp.sum(divergence * divergence)
        slopes = jnp.stack([central(penalty, 0), central(penalty, 1), central(penalty, 2)], axis=1)
        grad_vel = ((2.0 * misfit - slopes) / BATCH).astype(jnp.bfloat16)
        zero_w = jnp.zeros((C, C), jnp.float32)
        zero_q = jnp.zeros((C, 3), jnp.float32)
        sums, grad_slab = lax.scan(plane_backward, (zero_w, zero_q), (field, back, grad_vel))
        grads = forward_x(grad_slab[None], normalize_scale)
        grad_r = mode_grads(grads, spectrum)
        return ((total_sums[0] + grad_r, total_sums[1] + sums[0], total_sums[2] + sums[1], total_sums[3] + loss_sum), penalty)
    start_offset = (jnp.zeros((MX, MY * MZ, 2, C, C), jnp.float32), jnp.zeros((C, C), jnp.float32), jnp.zeros((C, 3), jnp.float32), jnp.zeros((), jnp.float32))
    total_sums, penalty_terms = lax.scan(single_example, start_offset, (fields, targets, multipliers))
    loss = (total_sums[3] / (BATCH * NX * NY * NZ)).reshape(1)
    return (penalty_terms, total_sums[0], total_sums[1] * normalize_scale, total_sums[2] * normalize_scale, loss)
```

```python
import functools
import math

import jax
import jax.numpy as jnp
import ml_dtypes
import numpy as np
from jax import lax
from jax.experimental import pallas as pl
from jax.experimental.pallas import tpu as pltpu
from jax.sharding import PartitionSpec as P

MX = 16
MY = 16
MZ = 16
ROWS = 16

penalty_weight = 0.5
precise = lax.Precision.HIGHEST
bf16 = jnp.bfloat16
f32 = jnp.float32
ROOT = math.sqrt(2.0 / math.pi)


def fourier_tables(length, count):
    position = np.arange(count)
    modes = np.where(position < count // 2, position, position - count)
    phase = np.mod(np.arange(length)[:, None] * modes[None, :], length)
    angle = phase.astype(np.float32) * np.float32(2.0 * math.pi / length)
    return np.cos(angle), np.sin(angle)


def halves(table):
    high = table.astype(ml_dtypes.bfloat16)
    low = (table - high.astype(np.float32)).astype(ml_dtypes.bfloat16)
    return high, low


def split(value):
    high = value.astype(bf16)
    return high, (value - high.astype(f32)).astype(bf16)


def dot(a, b):
    return jnp.dot(a, b, preferred_element_type=f32)


def dot_nt(a, b):
    return lax.dot_general(a, b, (((1,), (1,)), ((), ())), preferred_element_type=f32)


def dot_tn(a, b):
    return lax.dot_general(a, b, (((0,), (0,)), ((), ())), preferred_element_type=f32)


def plane_modes(load, count, ty, zt):
    parts = jnp.stack([dot(ty, load(c)) for c in range(count)], axis=0)
    turned = jnp.swapaxes(parts, 0, 1)
    nz = turned.shape[-1]
    real = turned[:MY].reshape(MY * count, nz)
    imag = turned[MY:].reshape(MY * count, nz)
    high, low = split(jnp.concatenate([real, imag], axis=1))
    both = dot_nt(zt, high)
    n = 2 * MZ
    return both[:n] + both[n:] + dot_nt(zt[:n], low)


def forward_body(f_ref, ty_ref, zt_ref, out_ref):
    count = f_ref.shape[1]
    out_ref[0] = plane_modes(lambda c: f_ref[0, c], count, ty_ref[...], zt_ref[...])


def tile_pair(ref, y0):
    count, nz = ref.shape[1], ref.shape[3]
    one = ref[0, :, pl.ds(y0, ROWS), :].reshape(count * ROWS, nz)
    two = ref[0, :, pl.ds(y0 + ROWS, ROWS), :].reshape(count * ROWS, nz)
    return jnp.concatenate([one, two], axis=1)


def put_pair(ref, y0, value):
    count, nz = ref.shape[1], ref.shape[3]
    ref[0, :, pl.ds(y0, ROWS), :] = value[:, :nz].reshape(count, ROWS, nz)
    ref[0, :, pl.ds(y0 + ROWS, ROWS), :] = value[:, nz:].reshape(count, ROWS, nz)


def middle_body(scale, f_ref, m_ref, zi_ref, yi_ref, kw_ref, kp_ref, pre_ref, vel_ref):
    count, ny, nz = f_ref.shape[1], f_ref.shape[2], f_ref.shape[3]
    high, low = split(m_ref[0])
    wave = dot_tn(jnp.concatenate([high, high, low], axis=0), zi_ref[...])
    turned = jnp.swapaxes(wave.reshape(MY, count, 2 * nz), 0, 1)
    yi = yi_ref[...]
    for o in range(0, count, 2):
        pair = [
            jnp.concatenate([turned[i, :, :nz], turned[i, :, nz:]], axis=0) for i in (o, o + 1)
        ]
        both = dot(yi, jnp.concatenate(pair, axis=1).astype(bf16))
        pre_ref[0, o] = both[:, :nz] * scale
        pre_ref[0, o + 1] = both[:, nz:] * scale

    @pl.loop(0, ny // (2 * ROWS))
    def _(step):
        y0 = pl.multiple_of(step * 2 * ROWS, 2 * ROWS)
        x = tile_pair(pre_ref, y0) + dot(kw_ref[...], tile_pair(f_ref, y0))
        put_pair(pre_ref, y0, x)
        t = jnp.tanh(ROOT * (x + 0.044715 * (x * x * x)))
        hidden = (x * (0.5 * (1.0 + t))).astype(bf16)
        put_pair(vel_ref, y0, dot(kp_ref[...], hidden))


def backward_body(
    f_ref, pre_ref, gv_ref, ty_ref, zt_ref, kpt_ref, out_ref, gw_ref, gq_ref, gp_ref
):
    count, ny, nz = f_ref.shape[1], f_ref.shape[2], f_ref.shape[3]

    @pl.when(pl.program_id(0) == 0)
    def _():
        gw_ref[...] = jnp.zeros_like(gw_ref)
        gq_ref[...] = jnp.zeros_like(gq_ref)

    @pl.loop(0, ny // (2 * ROWS))
    def _(step):
        y0 = pl.multiple_of(step * 2 * ROWS, 2 * ROWS)
        gv = tile_pair(gv_ref, y0)
        x = tile_pair(pre_ref, y0)
        xx = x * x
        t = jnp.tanh(ROOT * (x + 0.044715 * (xx * x)))
        cdf = 0.5 * (1.0 + t)
        hidden = (x * cdf).astype(bf16)
        slope = cdf + x * (0.5 * (1.0 - t * t)) * (ROOT + (3.0 * 0.044715 * ROOT) * xx)
        gp = (dot(kpt_ref[...], gv) * slope).astype(bf16)
        put_pair(gp_ref, y0, gp)
        gw_ref[...] += dot_nt(tile_pair(f_ref, y0), gp)
        gq_ref[...] += dot_nt(hidden, gv)

    out_ref[0] = plane_modes(lambda c: gp_ref[0, c], count, ty_ref[...], zt_ref[...])


def whole(shape):
    return pl.BlockSpec(shape, lambda i: (0,) * len(shape))


def plane(shape):
    return pl.BlockSpec((1,) + tuple(shape), lambda i: (i,) + (0,) * len(shape))


params = pltpu.CompilerParams(
    dimension_semantics=("arbitrary",), vmem_limit_bytes=56 * 1024 * 1024
)


def extended(value, axis_name):
    count = lax.axis_size(axis_name)
    up = [(i, (i + 1) % count) for i in range(count)]
    down = [(j, i) for i, j in up]
    before = lax.ppermute(value[-1:], axis_name, up)
    after = lax.ppermute(value[:1], axis_name, down)
    return jnp.concatenate([before, value, after], axis=0)


def central(values, axis):
    return (jnp.roll(values, -1, axis) - jnp.roll(values, 1, axis)) * 0.5


def local(fields, targets, multipliers, local_weight, proj_weight, spectral_weight):
    gx = lax.axis_size("gx")
    rep = lax.axis_size("rep")
    _, xl, C, NY, NZ = fields.shape
    NX = xl * gx
    PL = MY * MZ // gx
    scale = 1.0 / math.sqrt(NX * NY * NZ)
    fields, targets, multipliers = fields[0], targets[0], multipliers[0]

    cos_y, sin_y = fourier_tables(NY, MY)
    ty = jnp.asarray(np.concatenate([cos_y.T, -sin_y.T], 0).astype(ml_dtypes.bfloat16))
    yi = jnp.asarray(np.concatenate([cos_y, -sin_y], 1).astype(ml_dtypes.bfloat16))
    cos_z, sin_z = fourier_tables(NZ, MZ)
    zt = np.concatenate(
        [np.concatenate([cos_z.T, sin_z.T], 1), np.concatenate([-sin_z.T, cos_z.T], 1)], 0
    )
    zt = jnp.asarray(np.concatenate(halves(zt), 0))
    zi = np.concatenate(
        [np.concatenate([cos_z.T, sin_z.T], 1), np.concatenate([-sin_z.T, cos_z.T], 1)], 0
    )
    zi_high, zi_low = halves(zi)
    zi = jnp.asarray(np.concatenate([zi_high, zi_low, zi_high], 0))
    cos_x, sin_x = fourier_tables(NX, MX)
    xt = np.stack(
        [np.stack([cos_x.T, sin_x.T], 1), np.stack([-sin_x.T, cos_x.T], 1)], 1
    )
    xt = xt.reshape(MX, 2, 2, gx, xl).transpose(0, 1, 3, 2, 4).reshape(2 * MX, 2 * NX)
    x_forward = jnp.asarray(xt * np.float32(scale))
    x_back = jnp.asarray(np.ascontiguousarray(xt.T))

    eye = jnp.eye(ROWS, dtype=bf16)
    kw = jnp.kron(local_weight.T, eye)
    kp = jnp.kron(proj_weight.T, eye)
    kpt = jnp.kron(proj_weight, eye)

    modes_shape = jax.ShapeDtypeStruct((xl, 2 * MZ, MY * C), f32)
    field_spec = plane((C, NY, NZ))
    modes_spec = plane((2 * MZ, MY * C))
    vel_spec = plane((3, NY, NZ))

    def to_owner(slab):
        slab = slab.reshape(xl, 2, MZ, MY, C).transpose(3, 2, 1, 0, 4)
        slab = slab.reshape(gx, PL, 2, xl, C).transpose(0, 2, 3, 1, 4)
        slab = slab.reshape(gx, 2 * xl, PL * C)
        slab = lax.all_to_all(slab, "gx", split_axis=0, concat_axis=0, tiled=True)
        out = jnp.dot(x_forward, slab.reshape(2 * NX, PL * C), precision=precise)
        return out.reshape(MX, 2, PL, C)

    def to_planes(modes):
        out = jnp.dot(x_back, modes.reshape(2 * MX, PL * C), precision=precise)
        out = out.reshape(gx, 2 * xl, PL * C)
        out = lax.all_to_all(out, "gx", split_axis=0, concat_axis=0, tiled=True)
        out = out.reshape(gx, 2, xl, PL, C).transpose(0, 3, 1, 2, 4)
        out = out.reshape(MY, MZ, 2, xl, C).transpose(3, 2, 1, 0, 4)
        return out.reshape(xl, 2 * MZ, MY * C)

    def both_samples(modes):
        part = modes.reshape(rep, MX // rep, 2, PL, C)
        return lax.all_to_all(part, "rep", split_axis=0, concat_axis=0, tiled=True)

    slab = pl.pallas_call(
        forward_body,
        grid=(xl,),
        out_shape=modes_shape,
        in_specs=[field_spec, whole(ty.shape), whole(zt.shape)],
        out_specs=modes_spec,
        compiler_params=params,
    )(fields, ty, zt)
    spectrum = to_owner(slab)
    weights = lax.all_gather(spectral_weight, "rep", axis=0, tiled=True).astype(f32)
    w_re, w_im = weights[:, :, 0], weights[:, :, 1]
    s_re, s_im = spectrum[:, 0], spectrum[:, 1]

    def apply(w, s):
        return jnp.einsum("mpoc,mpc->mpo", w, s, precision=precise)

    product = jnp.stack(
        [apply(w_re, s_re) - apply(w_im, s_im), apply(w_re, s_im) + apply(w_im, s_re)], axis=1
    )
    wave = to_planes(product)
    spectra = both_samples(spectrum)

    pre, velocity = pl.pallas_call(
        functools.partial(middle_body, scale),
        grid=(xl,),
        out_shape=(
            jax.ShapeDtypeStruct((xl, C, NY, NZ), f32),
            jax.ShapeDtypeStruct((xl, 3, NY, NZ), f32),
        ),
        in_specs=[
            field_spec,
            modes_spec,
            whole(zi.shape),
            whole(yi.shape),
            whole(kw.shape),
            whole(kp.shape),
        ],
        out_specs=(field_spec, vel_spec),
        compiler_params=params,
    )(fields, wave, zi, yi, kw, kp)

    padded = extended(velocity[:, 0].astype(bf16), "gx").astype(f32)
    slope_x = (padded[2:] - padded[:-2]) * 0.5
    divergence = slope_x + central(velocity[:, 1], 1) + central(velocity[:, 2], 2)
    lam = multipliers.astype(f32) / 64.0
    penalty = lam + penalty_weight * divergence
    misfit = velocity - targets.astype(f32)
    loss_sum = (
        jnp.sum(misfit * misfit)
        + jnp.sum(lam * divergence)
        + 0.5 * penalty_weight * jnp.sum(divergence * divergence)
    )
    padded = extended(penalty.astype(bf16), "gx").astype(f32)
    pen_x = (padded[2:] - padded[:-2]) * 0.5
    slopes = jnp.stack([pen_x, central(penalty, 1), central(penalty, 2)], axis=1)
    grad_vel = ((2.0 * misfit - slopes) / rep).astype(bf16)

    wide = C * ROWS
    grad_slab, gw, gq = pl.pallas_call(
        backward_body,
        grid=(xl,),
        out_shape=(
            modes_shape,
            jax.ShapeDtypeStruct((wide, wide), f32),
            jax.ShapeDtypeStruct((wide, 3 * ROWS), f32),
        ),
        in_specs=[
            field_spec,
            field_spec,
            vel_spec,
            whole(ty.shape),
            whole(zt.shape),
            whole(kpt.shape),
        ],
        out_specs=(modes_spec, whole((wide, wide)), whole((wide, 3 * ROWS))),
        scratch_shapes=[pltpu.VMEM((1, C, NY, NZ), bf16)],
        compiler_params=params,
    )(fields, pre, grad_vel, ty, zt, kpt)

    grads = both_samples(to_owner(grad_slab))

    gather = jnp.asarray(np.kron(np.eye(C), np.ones((1, ROWS))).astype(np.float32))
    gather_q = jnp.asarray(np.kron(np.eye(3), np.ones((ROWS, 1))).astype(np.float32))
    mask = jnp.asarray(np.kron(np.ones((C, C)), np.eye(ROWS)).astype(np.float32))
    mask_q = jnp.asarray(np.kron(np.ones((C, 3)), np.eye(ROWS)).astype(np.float32))
    grad_w = jnp.dot(jnp.dot(gather, gw * mask, precision=precise), gather.T, precision=precise)
    grad_q = jnp.dot(jnp.dot(gather, gq * mask_q, precision=precise), gather_q, precision=precise)
    packed = jnp.concatenate([grad_w.reshape(-1), grad_q.reshape(-1), loss_sum.reshape(1)])
    packed = lax.psum(packed, ("gx", "rep"))
    grad_w = packed[: C * C].reshape(C, C) * scale
    grad_q = packed[C * C : C * C + 3 * C].reshape(C, 3) * scale
    loss = packed[-1:] / (rep * NX * NY * NZ)

    g_re, g_im = grads[:, :, 0], grads[:, :, 1]
    s_re, s_im = spectra[:, :, 0], spectra[:, :, 1]

    def outer(g, s):
        return jnp.sum(g[..., :, None] * s[..., None, :], axis=0)

    grad_r = jnp.stack(
        [outer(g_re, s_re) + outer(g_im, s_im), outer(g_im, s_re) - outer(g_re, s_im)], axis=2
    )
    return (penalty[None], grad_r, grad_w, grad_q, loss)


def solution(mesh):
    in_specs = (
        P(("grp", "rep"), "gx", None, None, None),
        P(("grp", "rep"), "gx", None, None, None),
        P(("grp", "rep"), "gx", None, None),
        P(),
        P(),
        P("rep", "gx", None, None, None),
    )
    out_specs = (
        P(("grp", "rep"), "gx", None, None),
        P(("grp", "rep"), "gx", None, None, None),
        P("grp", None),
        P("grp", None),
        P("grp"),
    )
    return jax.shard_map(local, mesh=mesh, in_specs=in_specs, out_specs=out_specs, check_vma=False)
```

```python
import functools
import math

import jax
import jax.numpy as jnp
import ml_dtypes
import numpy as np
from jax import lax
from jax.experimental import pallas as pl
from jax.experimental.pallas import tpu as pltpu
from jax.sharding import PartitionSpec as P

MX = 16
MY = 16
MZ = 16
ROWS = 16

penalty_weight = 0.5
precise = lax.Precision.HIGHEST
bf16 = jnp.bfloat16
f32 = jnp.float32
ROOT = math.sqrt(2.0 / math.pi)


def fourier_tables(length, count):
    position = np.arange(count)
    modes = np.where(position < count // 2, position, position - count)
    phase = np.mod(np.arange(length)[:, None] * modes[None, :], length)
    angle = phase.astype(np.float32) * np.float32(2.0 * math.pi / length)
    return np.cos(angle), np.sin(angle)


def halves(table):
    high = table.astype(ml_dtypes.bfloat16)
    low = (table - high.astype(np.float32)).astype(ml_dtypes.bfloat16)
    return high, low


def split(value):
    high = value.astype(bf16)
    return high, (value - high.astype(f32)).astype(bf16)


def dot(a, b):
    return jnp.dot(a, b, preferred_element_type=f32)


def dot_nt(a, b):
    return lax.dot_general(a, b, (((1,), (1,)), ((), ())), preferred_element_type=f32)


def dot_tn(a, b):
    return lax.dot_general(a, b, (((0,), (0,)), ((), ())), preferred_element_type=f32)


def plane_modes(load, count, ty, zt):
    parts = jnp.stack([dot(ty, load(c)) for c in range(count)], axis=0)
    turned = jnp.swapaxes(parts, 0, 1)
    nz = turned.shape[-1]
    real = turned[:MY].reshape(MY * count, nz)
    imag = turned[MY:].reshape(MY * count, nz)
    high, low = split(jnp.concatenate([real, imag], axis=1))
    both = dot_nt(zt, high)
    n = 2 * MZ
    return both[:n] + both[n:] + dot_nt(zt[:n], low)


def store_modes(out_ref, modes):
    if len(out_ref.shape) == 3:
        out_ref[0] = modes
        return
    owners, _, _, high, lanes = out_ref.shape
    width = modes.shape[1] // owners
    rows = 2 * high
    for d in range(owners):
        parts = [
            modes[j * rows : (j + 1) * rows, d * width : (d + 1) * width]
            for j in range(lanes // width)
        ]
        out_ref[d, 0] = jnp.concatenate(parts, axis=1).reshape(2, high, lanes)


def load_modes(m_ref, columns):
    if len(m_ref.shape) == 3:
        return m_ref[0]
    owners, _, _, high, lanes = m_ref.shape
    width = columns // owners
    blocks = [m_ref[d, 0].reshape(2 * high, lanes) for d in range(owners)]
    rows = [
        jnp.concatenate([block[:, j * width : (j + 1) * width] for block in blocks], axis=1)
        for j in range(lanes // width)
    ]
    return jnp.concatenate(rows, axis=0)


def x_forward_body(slab_ref, table_ref, out_ref):
    count = out_ref.shape[0]
    xl = table_ref.shape[1] // (2 * slab_ref.shape[0])
    value = slab_ref[:, :xl].reshape(table_ref.shape[1], count, out_ref.shape[2])
    turned = jnp.swapaxes(value, 0, 1)
    for k in range(count):
        out_ref[k] = jnp.dot(
            table_ref[...], turned[k], precision=precise, preferred_element_type=f32
        )


def x_back_body(modes_ref, table_ref, out_ref):
    parts = [
        jnp.dot(table_ref[...], modes_ref[k], precision=precise, preferred_element_type=f32)
        for k in range(modes_ref.shape[0])
    ]
    turned = jnp.swapaxes(jnp.stack(parts, axis=0), 0, 1)
    out_ref[...] = turned.reshape(out_ref.shape)


def forward_body(f_ref, ty_ref, zt_ref, out_ref):
    count = f_ref.shape[1]
    store_modes(out_ref, plane_modes(lambda c: f_ref[0, c], count, ty_ref[...], zt_ref[...]))


def tile_pair(ref, y0):
    count, nz = ref.shape[1], ref.shape[3]
    one = ref[0, :, pl.ds(y0, ROWS), :].reshape(count * ROWS, nz)
    two = ref[0, :, pl.ds(y0 + ROWS, ROWS), :].reshape(count * ROWS, nz)
    return jnp.concatenate([one, two], axis=1)


def put_pair(ref, y0, value):
    count, nz = ref.shape[1], ref.shape[3]
    ref[0, :, pl.ds(y0, ROWS), :] = value[:, :nz].reshape(count, ROWS, nz)
    ref[0, :, pl.ds(y0 + ROWS, ROWS), :] = value[:, nz:].reshape(count, ROWS, nz)


def middle_body(scale, f_ref, m_ref, zi_ref, yi_ref, kw_ref, kp_ref, pre_ref, vel_ref):
    count, ny, nz = f_ref.shape[1], f_ref.shape[2], f_ref.shape[3]
    high, low = split(load_modes(m_ref, MY * count))
    wave = dot_tn(jnp.concatenate([high, high, low], axis=0), zi_ref[...])
    turned = jnp.swapaxes(wave.reshape(MY, count, 2 * nz), 0, 1)
    yi = yi_ref[...]
    for o in range(0, count, 2):
        pair = [
            jnp.concatenate([turned[i, :, :nz], turned[i, :, nz:]], axis=0) for i in (o, o + 1)
        ]
        both = dot(yi, jnp.concatenate(pair, axis=1).astype(bf16))
        pre_ref[0, o] = both[:, :nz] * scale
        pre_ref[0, o + 1] = both[:, nz:] * scale

    @pl.loop(0, ny // (2 * ROWS))
    def _(step):
        y0 = pl.multiple_of(step * 2 * ROWS, 2 * ROWS)
        x = tile_pair(pre_ref, y0) + dot(kw_ref[...], tile_pair(f_ref, y0))
        put_pair(pre_ref, y0, x)
        t = jnp.tanh(ROOT * (x + 0.044715 * (x * x * x)))
        hidden = (x * (0.5 * (1.0 + t))).astype(bf16)
        put_pair(vel_ref, y0, dot(kp_ref[...], hidden))


def backward_body(
    f_ref, pre_ref, gv_ref, ty_ref, zt_ref, kpt_ref, out_ref, gw_ref, gq_ref, gp_ref
):
    count, ny, nz = f_ref.shape[1], f_ref.shape[2], f_ref.shape[3]

    @pl.when(pl.program_id(0) == 0)
    def _():
        gw_ref[...] = jnp.zeros_like(gw_ref)
        gq_ref[...] = jnp.zeros_like(gq_ref)

    @pl.loop(0, ny // (2 * ROWS))
    def _(step):
        y0 = pl.multiple_of(step * 2 * ROWS, 2 * ROWS)
        gv = tile_pair(gv_ref, y0)
        x = tile_pair(pre_ref, y0)
        xx = x * x
        t = jnp.tanh(ROOT * (x + 0.044715 * (xx * x)))
        cdf = 0.5 * (1.0 + t)
        hidden = (x * cdf).astype(bf16)
        slope = cdf + x * (0.5 * (1.0 - t * t)) * (ROOT + (3.0 * 0.044715 * ROOT) * xx)
        gp = (dot(kpt_ref[...], gv) * slope).astype(bf16)
        put_pair(gp_ref, y0, gp)
        gw_ref[...] += dot_nt(tile_pair(f_ref, y0), gp)
        gq_ref[...] += dot_nt(hidden, gv)

    store_modes(out_ref, plane_modes(lambda c: gp_ref[0, c], count, ty_ref[...], zt_ref[...]))


def whole(shape):
    return pl.BlockSpec(shape, lambda i: (0,) * len(shape))


def plane(shape):
    return pl.BlockSpec((1,) + tuple(shape), lambda i: (i,) + (0,) * len(shape))


params = pltpu.CompilerParams(
    dimension_semantics=("arbitrary",), vmem_limit_bytes=56 * 1024 * 1024
)


def extended(value, axis_name):
    count = lax.axis_size(axis_name)
    up = [(i, (i + 1) % count) for i in range(count)]
    down = [(j, i) for i, j in up]
    before = lax.ppermute(value[-1:], axis_name, up)
    after = lax.ppermute(value[:1], axis_name, down)
    return jnp.concatenate([before, value, after], axis=0)


def central(values, axis):
    return (jnp.roll(values, -1, axis) - jnp.roll(values, 1, axis)) * 0.5


def local(fields, targets, multipliers, local_weight, proj_weight, spectral_weight):
    gx = lax.axis_size("gx")
    rep = lax.axis_size("rep")
    _, xl, C, NY, NZ = fields.shape
    NX = xl * gx
    PL = MY * MZ // gx
    scale = 1.0 / math.sqrt(NX * NY * NZ)
    fields, targets, multipliers = fields[0], targets[0], multipliers[0]

    cos_y, sin_y = fourier_tables(NY, MY)
    ty = jnp.asarray(np.concatenate([cos_y.T, -sin_y.T], 0).astype(ml_dtypes.bfloat16))
    yi = jnp.asarray(np.concatenate([cos_y, -sin_y], 1).astype(ml_dtypes.bfloat16))
    cos_z, sin_z = fourier_tables(NZ, MZ)
    zt = np.concatenate(
        [np.concatenate([cos_z.T, sin_z.T], 1), np.concatenate([-sin_z.T, cos_z.T], 1)], 0
    )
    direct = MY % gx == 0 and 128 % (MY // gx * C) == 0
    KY = MY // gx if direct else 0
    PK = 128 // (KY * C) if direct else 1
    HZ = MZ // PK
    order = np.arange(2 * MZ).reshape(2, HZ, PK).transpose(2, 0, 1).reshape(-1)
    zt = zt[order]
    zi_high, zi_low = halves(zt)
    zt = jnp.asarray(np.concatenate([zi_high, zi_low], 0))
    zi = jnp.asarray(np.concatenate([zi_high, zi_low, zi_high], 0))
    cos_x, sin_x = fourier_tables(NX, MX)
    xt = np.stack(
        [np.stack([cos_x.T, sin_x.T], 1), np.stack([-sin_x.T, cos_x.T], 1)], 1
    )
    xt = xt.reshape(MX, 2, 2, gx, xl).transpose((0, 1, 3, 4, 2) if direct else (0, 1, 3, 2, 4))
    xt = xt.reshape(2 * MX, 2 * NX)
    x_forward = jnp.asarray(xt * np.float32(scale))
    x_back = jnp.asarray(np.ascontiguousarray(xt.T))

    eye = jnp.eye(ROWS, dtype=bf16)
    kw = jnp.kron(local_weight.T, eye)
    kp = jnp.kron(proj_weight.T, eye)
    kpt = jnp.kron(proj_weight, eye)

    field_spec = plane((C, NY, NZ))
    EX = -(-C // (2 * HZ)) if direct else 0
    if direct:
        modes_shape = jax.ShapeDtypeStruct((gx, xl, 2, HZ, 128), f32)
        sums_shape = jax.ShapeDtypeStruct((gx, xl + EX, 2, HZ, 128), f32)
        modes_spec = pl.BlockSpec((gx, 1, 2, HZ, 128), lambda i: (0, i, 0, 0, 0))
    else:
        modes_shape = jax.ShapeDtypeStruct((xl, 2 * MZ, MY * C), f32)
        sums_shape = modes_shape
        modes_spec = plane((2 * MZ, MY * C))
    vel_spec = plane((3, NY, NZ))

    def exchange(slab):
        return lax.all_to_all(slab, "gx", split_axis=0, concat_axis=0, tiled=True)

    def x_modes(slab):
        out = pl.pallas_call(
            x_forward_body,
            out_shape=jax.ShapeDtypeStruct((HZ, 2 * MX, 128), f32),
            compiler_params=pltpu.CompilerParams(vmem_limit_bytes=32 * 1024 * 1024),
        )(slab, x_forward)
        out = out.reshape(HZ, MX, 2, PK, KY, C).transpose(1, 2, 4, 0, 3, 5)
        return out.reshape(MX, 2, PL, C)

    def to_owner(slab):
        if direct:
            return x_modes(exchange(slab))
        slab = slab.reshape(xl, 2, MZ, MY, C).transpose(3, 2, 1, 0, 4)
        slab = slab.reshape(gx, PL, 2, xl, C).transpose(0, 2, 3, 1, 4)
        slab = slab.reshape(gx, 2 * xl, PL * C)
        slab = lax.all_to_all(slab, "gx", split_axis=0, concat_axis=0, tiled=True)
        out = jnp.dot(x_forward, slab.reshape(2 * NX, PL * C), precision=precise)
        return out.reshape(MX, 2, PL, C)

    def to_planes(modes):
        if direct:
            out = modes.reshape(MX, 2, KY, HZ, PK, C).transpose(3, 0, 1, 4, 2, 5)
            out = pl.pallas_call(
                x_back_body,
                out_shape=modes_shape,
                compiler_params=pltpu.CompilerParams(vmem_limit_bytes=32 * 1024 * 1024),
            )(out.reshape(HZ, 2 * MX, 128), x_back)
            return exchange(out)
        out = jnp.dot(x_back, modes.reshape(2 * MX, PL * C), precision=precise)
        out = out.reshape(gx, 2 * xl, PL * C)
        out = lax.all_to_all(out, "gx", split_axis=0, concat_axis=0, tiled=True)
        out = out.reshape(gx, 2, xl, PL, C).transpose(0, 3, 1, 2, 4)
        out = out.reshape(MY, MZ, 2, xl, C).transpose(3, 2, 1, 0, 4)
        return out.reshape(xl, 2 * MZ, MY * C)

    def both_samples(modes):
        part = modes.reshape(rep, MX // rep, 2, PL, C)
        return lax.all_to_all(part, "rep", split_axis=0, concat_axis=0, tiled=True)

    slab = pl.pallas_call(
        forward_body,
        grid=(xl,),
        out_shape=modes_shape,
        in_specs=[field_spec, whole(ty.shape), whole(zt.shape)],
        out_specs=modes_spec,
        compiler_params=params,
    )(fields, ty, zt)
    spectrum = to_owner(slab)
    weights = lax.all_gather(spectral_weight, "rep", axis=0, tiled=True)
    weights = weights.transpose(2, 3, 4, 0, 1).reshape(2, C, C, MX * PL)
    w_re, w_im = lax.optimization_barrier(weights).astype(f32)
    turned = spectrum.transpose(1, 3, 0, 2).reshape(2, 1, C, MX * PL)
    s_re, s_im = turned[0], turned[1]
    product = jnp.stack(
        [jnp.sum(w_re * s_re - w_im * s_im, axis=1), jnp.sum(w_re * s_im + w_im * s_re, axis=1)]
    )
    product = product.reshape(2, C, MX, PL).transpose(2, 0, 3, 1)
    wave = to_planes(product)
    spectra = both_samples(spectrum)

    pre, velocity = pl.pallas_call(
        functools.partial(middle_body, scale),
        grid=(xl,),
        out_shape=(
            jax.ShapeDtypeStruct((xl, C, NY, NZ), f32),
            jax.ShapeDtypeStruct((xl, 3, NY, NZ), f32),
        ),
        in_specs=[
            field_spec,
            modes_spec,
            whole(zi.shape),
            whole(yi.shape),
            whole(kw.shape),
            whole(kp.shape),
        ],
        out_specs=(field_spec, vel_spec),
        compiler_params=params,
    )(fields, wave, zi, yi, kw, kp)

    padded = extended(velocity[:, 0].astype(bf16), "gx").astype(f32)
    slope_x = (padded[2:] - padded[:-2]) * 0.5
    divergence = slope_x + central(velocity[:, 1], 1) + central(velocity[:, 2], 2)
    lam = multipliers.astype(f32) / 64.0
    penalty = lam + penalty_weight * divergence
    misfit = velocity - targets.astype(f32)
    loss_sum = (
        jnp.sum(misfit * misfit)
        + jnp.sum(lam * divergence)
        + 0.5 * penalty_weight * jnp.sum(divergence * divergence)
    )
    padded = extended(penalty.astype(bf16), "gx").astype(f32)
    pen_x = (padded[2:] - padded[:-2]) * 0.5
    slopes = jnp.stack([pen_x, central(penalty, 1), central(penalty, 2)], axis=1)
    grad_vel = ((2.0 * misfit - slopes) / rep).astype(bf16)

    wide = C * ROWS
    grad_slab, gw, gq = pl.pallas_call(
        backward_body,
        grid=(xl,),
        out_shape=(
            sums_shape,
            jax.ShapeDtypeStruct((wide, wide), f32),
            jax.ShapeDtypeStruct((wide, 3 * ROWS), f32),
        ),
        in_specs=[
            field_spec,
            field_spec,
            vel_spec,
            whole(ty.shape),
            whole(zt.shape),
            whole(kpt.shape),
        ],
        out_specs=(modes_spec, whole((wide, wide)), whole((wide, 3 * ROWS))),
        scratch_shapes=[pltpu.VMEM((1, C, NY, NZ), bf16)],
        compiler_params=params,
    )(fields, pre, grad_vel, ty, zt, kpt)

    gather = jnp.asarray(np.kron(np.eye(C), np.ones((1, ROWS))).astype(np.float32))
    gather_q = jnp.asarray(np.kron(np.eye(3), np.ones((ROWS, 1))).astype(np.float32))
    mask = jnp.asarray(np.kron(np.ones((C, C)), np.eye(ROWS)).astype(np.float32))
    mask_q = jnp.asarray(np.kron(np.ones((C, 3)), np.eye(ROWS)).astype(np.float32))
    grad_w = jnp.dot(jnp.dot(gather, gw * mask, precision=precise), gather.T, precision=precise)
    grad_q = jnp.dot(jnp.dot(gather, gq * mask_q, precision=precise), gather_q, precision=precise)
    if direct:
        last = jnp.broadcast_to(loss_sum.reshape(1, 1), (C, 1))
        packed = jnp.concatenate([grad_w, grad_q, last], axis=1)
        packed = jnp.pad(packed, ((0, 0), (0, 128 - C - 4)))
        packed = jnp.pad(packed.reshape(-1), (0, EX * 2 * HZ * 128 - C * 128))
        packed = jnp.broadcast_to(packed.reshape(1, EX, 2, HZ, 128), (gx, EX, 2, HZ, 128))
        slab = exchange(lax.dynamic_update_slice(grad_slab, packed, (0, xl, 0, 0, 0)))
        grads = x_modes(slab)
        sums = jnp.sum(slab[:, xl:], axis=0).reshape(-1)
        both = jnp.concatenate(
            [grads.reshape(rep, -1), jnp.broadcast_to(sums[None], (rep, sums.size))], axis=1
        )
        both = lax.all_to_all(both, "rep", split_axis=0, concat_axis=0, tiled=True)
        size = grads.size // rep
        grads = both[:, :size].reshape(rep, MX // rep, 2, PL, C)
        sums = jnp.sum(both[:, size:], axis=0)[: C * 128].reshape(C, 128)
        grad_w, grad_q, loss = sums[:, :C], sums[:, C : C + 3], sums[0, C + 3 : C + 4]
    else:
        grads = both_samples(to_owner(grad_slab))
        packed = jnp.concatenate([grad_w.reshape(-1), grad_q.reshape(-1), loss_sum.reshape(1)])
        packed = lax.psum(packed, ("gx", "rep"))
        grad_w = packed[: C * C].reshape(C, C)
        grad_q = packed[C * C : C * C + 3 * C].reshape(C, 3)
        loss = packed[-1:]
    loss = loss / (rep * NX * NY * NZ)

    g_re, g_im = grads[:, :, 0], grads[:, :, 1]
    across = jnp.stack([jnp.stack([g_re, g_im], 3), jnp.stack([g_im, -g_re], 3)], 1)
    terms = [
        across[b, t][..., None] * spectra[b, :, t][:, :, None, None, :]
        for b in range(rep)
        for t in range(2)
    ]
    grad_r = sum(terms[1:], terms[0])
    return (penalty[None], grad_r, grad_w * scale, grad_q * scale, loss)


def solution(mesh):
    in_specs = (
        P(("grp", "rep"), "gx", None, None, None),
        P(("grp", "rep"), "gx", None, None, None),
        P(("grp", "rep"), "gx", None, None),
        P(),
        P(),
        P("rep", "gx", None, None, None),
    )
    out_specs = (
        P(("grp", "rep"), "gx", None, None),
        P(("grp", "rep"), "gx", None, None, None),
        P("grp", None),
        P("grp", None),
        P("grp"),
    )
    return jax.shard_map(local, mesh=mesh, in_specs=in_specs, out_specs=out_specs, check_vma=False)
```

```python
import functools
import math

import jax
import jax.numpy as jnp
import ml_dtypes
import numpy as np
from jax import lax
from jax.experimental import pallas as pl
from jax.experimental.pallas import tpu as pltpu
from jax.sharding import PartitionSpec as P

MX = 16
MY = 16
MZ = 16
ROWS = 16

penalty_weight = 0.5
precise = lax.Precision.HIGHEST
bf16 = jnp.bfloat16
f32 = jnp.float32
ROOT = math.sqrt(2.0 / math.pi)


def fourier_tables(length, count):
    position = np.arange(count)
    modes = np.where(position < count // 2, position, position - count)
    phase = np.mod(np.arange(length)[:, None] * modes[None, :], length)
    angle = phase.astype(np.float32) * np.float32(2.0 * math.pi / length)
    return np.cos(angle), np.sin(angle)


def halves(table):
    high = table.astype(ml_dtypes.bfloat16)
    low = (table - high.astype(np.float32)).astype(ml_dtypes.bfloat16)
    return high, low


def split(value):
    high = value.astype(bf16)
    return high, (value - high.astype(f32)).astype(bf16)


def dot(a, b):
    return jnp.dot(a, b, preferred_element_type=f32)


def dot_nt(a, b):
    return lax.dot_general(a, b, (((1,), (1,)), ((), ())), preferred_element_type=f32)


def dot_tn(a, b):
    return lax.dot_general(a, b, (((0,), (0,)), ((), ())), preferred_element_type=f32)


def plane_modes(load, count, ty, zt):
    parts = []
    for c in range(0, count, 2):
        pair = dot(ty, jnp.concatenate([load(c), load(c + 1)], axis=1))
        nz = pair.shape[1] // 2
        parts += [pair[:, :nz], pair[:, nz:]]
    turned = jnp.swapaxes(jnp.stack(parts, axis=0), 0, 1)
    real = turned[:MY].reshape(MY * count, nz)
    imag = turned[MY:].reshape(MY * count, nz)
    high, low = split(jnp.concatenate([real, imag], axis=1))
    both = dot_nt(zt, high)
    n = 2 * MZ
    return both[:n] + both[n:] + dot_nt(zt[:n], low)


def store_modes(out_ref, modes):
    if len(out_ref.shape) == 3:
        out_ref[0] = modes
        return
    owners, _, _, high, lanes = out_ref.shape
    width = modes.shape[1] // owners
    rows = 2 * high
    for d in range(owners):
        parts = [
            modes[j * rows : (j + 1) * rows, d * width : (d + 1) * width]
            for j in range(lanes // width)
        ]
        out_ref[d, 0] = jnp.concatenate(parts, axis=1).reshape(2, high, lanes)


def load_modes(m_ref, columns):
    if len(m_ref.shape) == 3:
        return m_ref[0]
    owners, _, _, high, lanes = m_ref.shape
    width = columns // owners
    blocks = [m_ref[d, 0].reshape(2 * high, lanes) for d in range(owners)]
    rows = [
        jnp.concatenate([block[:, j * width : (j + 1) * width] for block in blocks], axis=1)
        for j in range(lanes // width)
    ]
    return jnp.concatenate(rows, axis=0)


def x_forward_body(slab_ref, table_ref, out_ref):
    count = out_ref.shape[0]
    xl = table_ref.shape[1] // (2 * slab_ref.shape[0])
    value = slab_ref[:, :xl].reshape(table_ref.shape[1], count, out_ref.shape[2])
    turned = jnp.swapaxes(value, 0, 1)
    for k in range(count):
        out_ref[k] = jnp.dot(
            table_ref[...], turned[k], precision=precise, preferred_element_type=f32
        )


def x_back_body(modes_ref, table_ref, out_ref):
    parts = [
        jnp.dot(table_ref[...], modes_ref[k], precision=precise, preferred_element_type=f32)
        for k in range(modes_ref.shape[0])
    ]
    turned = jnp.swapaxes(jnp.stack(parts, axis=0), 0, 1)
    out_ref[...] = turned.reshape(out_ref.shape)


def forward_body(f_ref, ty_ref, zt_ref, out_ref):
    count = f_ref.shape[1]
    store_modes(out_ref, plane_modes(lambda c: f_ref[0, c], count, ty_ref[...], zt_ref[...]))


def tile_pair(ref, y0):
    count, nz = ref.shape[1], ref.shape[3]
    one = ref[0, :, pl.ds(y0, ROWS), :].reshape(count * ROWS, nz)
    two = ref[0, :, pl.ds(y0 + ROWS, ROWS), :].reshape(count * ROWS, nz)
    return jnp.concatenate([one, two], axis=1)


def put_pair(ref, y0, value):
    count, nz = ref.shape[1], ref.shape[3]
    ref[0, :, pl.ds(y0, ROWS), :] = value[:, :nz].reshape(count, ROWS, nz)
    ref[0, :, pl.ds(y0 + ROWS, ROWS), :] = value[:, nz:].reshape(count, ROWS, nz)


def middle_body(scale, f_ref, m_ref, zi_ref, yi_ref, kw_ref, kp_ref, pre_ref, vel_ref):
    count, ny, nz = f_ref.shape[1], f_ref.shape[2], f_ref.shape[3]
    high, low = split(load_modes(m_ref, MY * count))
    wave = dot_tn(jnp.concatenate([high, high, low], axis=0), zi_ref[...])
    turned = jnp.swapaxes(wave.reshape(MY, count, 2 * nz), 0, 1)
    yi = yi_ref[...]
    for o in range(0, count, 2):
        pair = [
            jnp.concatenate([turned[i, :, :nz], turned[i, :, nz:]], axis=0) for i in (o, o + 1)
        ]
        both = dot(yi, jnp.concatenate(pair, axis=1).astype(bf16))
        pre_ref[0, o] = both[:, :nz] * scale
        pre_ref[0, o + 1] = both[:, nz:] * scale

    for y0 in range(0, ny, 2 * ROWS):
        x = tile_pair(pre_ref, y0) + dot(kw_ref[...], tile_pair(f_ref, y0))
        put_pair(pre_ref, y0, x)
        t = jnp.tanh(x * (ROOT + (0.044715 * ROOT) * (x * x)))
        half = 0.5 * x
        hidden = (half + half * t).astype(bf16)
        put_pair(vel_ref, y0, dot(kp_ref[...], hidden))


def backward_body(
    f_ref, pre_ref, gv_ref, ty_ref, zt_ref, kpt_ref, out_ref, gw_ref, gq_ref, gp_ref
):
    count, ny, nz = f_ref.shape[1], f_ref.shape[2], f_ref.shape[3]

    @pl.when(pl.program_id(0) == 0)
    def _():
        gw_ref[...] = jnp.zeros_like(gw_ref)
        gq_ref[...] = jnp.zeros_like(gq_ref)

    hiddens, grads, fields, slopes = [], [], [], []
    for y0 in range(0, ny, 2 * ROWS):
        gv = tile_pair(gv_ref, y0)
        x = tile_pair(pre_ref, y0)
        cubic = (0.044715 * ROOT) * (x * x)
        t = jnp.tanh(x * (ROOT + cubic))
        cdf = 0.5 + 0.5 * t
        hidden = (x * cdf).astype(bf16)
        slope = cdf + (x * (ROOT + 3.0 * cubic)) * (0.5 - 0.5 * (t * t))
        gp = (dot(kpt_ref[...], gv) * slope).astype(bf16)
        put_pair(gp_ref, y0, gp)
        hiddens.append(hidden)
        grads.append(gp)
        slopes.append(gv)
        fields.append(tile_pair(f_ref, y0))
    gw_ref[...] += dot_nt(jnp.concatenate(fields, axis=1), jnp.concatenate(grads, axis=1))
    gq_ref[...] += dot_nt(jnp.concatenate(hiddens, axis=1), jnp.concatenate(slopes, axis=1))

    store_modes(out_ref, plane_modes(lambda c: gp_ref[0, c], count, ty_ref[...], zt_ref[...]))


def whole(shape):
    return pl.BlockSpec(shape, lambda i: (0,) * len(shape))


def plane(shape):
    return pl.BlockSpec((1,) + tuple(shape), lambda i: (i,) + (0,) * len(shape))


params = pltpu.CompilerParams(
    dimension_semantics=("arbitrary",), vmem_limit_bytes=56 * 1024 * 1024
)


def extended(value, axis_name):
    count = lax.axis_size(axis_name)
    up = [(i, (i + 1) % count) for i in range(count)]
    down = [(j, i) for i, j in up]
    before = lax.ppermute(value[-1:], axis_name, up)
    after = lax.ppermute(value[:1], axis_name, down)
    return jnp.concatenate([before, value, after], axis=0)


def central(values, axis):
    return (jnp.roll(values, -1, axis) - jnp.roll(values, 1, axis)) * 0.5


def local(fields, targets, multipliers, local_weight, proj_weight, spectral_weight):
    gx = lax.axis_size("gx")
    rep = lax.axis_size("rep")
    _, xl, C, NY, NZ = fields.shape
    NX = xl * gx
    PL = MY * MZ // gx
    scale = 1.0 / math.sqrt(NX * NY * NZ)
    fields, targets, multipliers = fields[0], targets[0], multipliers[0]

    cos_y, sin_y = fourier_tables(NY, MY)
    ty = jnp.asarray(np.concatenate([cos_y.T, -sin_y.T], 0).astype(ml_dtypes.bfloat16))
    yi = jnp.asarray(np.concatenate([cos_y, -sin_y], 1).astype(ml_dtypes.bfloat16))
    cos_z, sin_z = fourier_tables(NZ, MZ)
    zt = np.concatenate(
        [np.concatenate([cos_z.T, sin_z.T], 1), np.concatenate([-sin_z.T, cos_z.T], 1)], 0
    )
    direct = MY % gx == 0 and 128 % (MY // gx * C) == 0
    KY = MY // gx if direct else 0
    PK = 128 // (KY * C) if direct else 1
    HZ = MZ // PK
    order = np.arange(2 * MZ).reshape(2, HZ, PK).transpose(2, 0, 1).reshape(-1)
    zt = zt[order]
    zi_high, zi_low = halves(zt)
    zt = jnp.asarray(np.concatenate([zi_high, zi_low], 0))
    zi = jnp.asarray(np.concatenate([zi_high, zi_low, zi_high], 0))
    cos_x, sin_x = fourier_tables(NX, MX)
    xt = np.stack(
        [np.stack([cos_x.T, sin_x.T], 1), np.stack([-sin_x.T, cos_x.T], 1)], 1
    )
    xt = xt.reshape(MX, 2, 2, gx, xl).transpose((0, 1, 3, 4, 2) if direct else (0, 1, 3, 2, 4))
    xt = xt.reshape(2 * MX, 2 * NX)
    x_forward = jnp.asarray(xt * np.float32(scale))
    x_back = jnp.asarray(np.ascontiguousarray(xt.T))

    eye = jnp.eye(ROWS, dtype=bf16)
    kw = jnp.kron(local_weight.T, eye)
    kp = jnp.kron(proj_weight.T, eye)
    kpt = jnp.kron(proj_weight, eye)

    field_spec = plane((C, NY, NZ))
    EX = -(-C // (2 * HZ)) if direct else 0
    if direct:
        modes_shape = jax.ShapeDtypeStruct((gx, xl, 2, HZ, 128), f32)
        sums_shape = jax.ShapeDtypeStruct((gx, xl + EX, 2, HZ, 128), f32)
        modes_spec = pl.BlockSpec((gx, 1, 2, HZ, 128), lambda i: (0, i, 0, 0, 0))
    else:
        modes_shape = jax.ShapeDtypeStruct((xl, 2 * MZ, MY * C), f32)
        sums_shape = modes_shape
        modes_spec = plane((2 * MZ, MY * C))
    vel_spec = plane((3, NY, NZ))

    def exchange(slab):
        return lax.all_to_all(slab, "gx", split_axis=0, concat_axis=0, tiled=True)

    def x_modes(slab):
        out = pl.pallas_call(
            x_forward_body,
            out_shape=jax.ShapeDtypeStruct((HZ, 2 * MX, 128), f32),
            compiler_params=pltpu.CompilerParams(vmem_limit_bytes=32 * 1024 * 1024),
        )(slab, x_forward)
        out = out.reshape(HZ, MX, 2, PK, KY, C).transpose(1, 2, 4, 0, 3, 5)
        return out.reshape(MX, 2, PL, C)

    def to_owner(slab):
        if direct:
            return x_modes(exchange(slab))
        slab = slab.reshape(xl, 2, MZ, MY, C).transpose(3, 2, 1, 0, 4)
        slab = slab.reshape(gx, PL, 2, xl, C).transpose(0, 2, 3, 1, 4)
        slab = slab.reshape(gx, 2 * xl, PL * C)
        slab = lax.all_to_all(slab, "gx", split_axis=0, concat_axis=0, tiled=True)
        out = jnp.dot(x_forward, slab.reshape(2 * NX, PL * C), precision=precise)
        return out.reshape(MX, 2, PL, C)

    def to_planes(modes):
        if direct:
            out = modes.reshape(MX, 2, KY, HZ, PK, C).transpose(3, 0, 1, 4, 2, 5)
            out = pl.pallas_call(
                x_back_body,
                out_shape=modes_shape,
                compiler_params=pltpu.CompilerParams(vmem_limit_bytes=32 * 1024 * 1024),
            )(out.reshape(HZ, 2 * MX, 128), x_back)
            return exchange(out)
        out = jnp.dot(x_back, modes.reshape(2 * MX, PL * C), precision=precise)
        out = out.reshape(gx, 2 * xl, PL * C)
        out = lax.all_to_all(out, "gx", split_axis=0, concat_axis=0, tiled=True)
        out = out.reshape(gx, 2, xl, PL, C).transpose(0, 3, 1, 2, 4)
        out = out.reshape(MY, MZ, 2, xl, C).transpose(3, 2, 1, 0, 4)
        return out.reshape(xl, 2 * MZ, MY * C)

    def both_samples(modes):
        part = modes.reshape(rep, MX // rep, 2, PL, C)
        return lax.all_to_all(part, "rep", split_axis=0, concat_axis=0, tiled=True)

    slab = pl.pallas_call(
        forward_body,
        grid=(xl,),
        out_shape=modes_shape,
        in_specs=[field_spec, whole(ty.shape), whole(zt.shape)],
        out_specs=modes_spec,
        compiler_params=params,
    )(fields, ty, zt)
    slab, weights = lax.optimization_barrier((slab, spectral_weight))
    weights = weights.transpose(2, 3, 4, 0, 1).reshape(1, 2, C, C, MX // rep * PL)
    weights = lax.all_gather(weights, "rep", axis=0, tiled=True)
    spectrum = to_owner(slab)
    KX = MX // rep
    turned = spectrum.reshape(rep, KX, 2, PL, C).transpose(0, 2, 4, 1, 3)
    turned = turned.reshape(rep, 2, 1, C, KX * PL)
    w_re, w_im = weights[:, 0].astype(f32), weights[:, 1].astype(f32)
    s_re, s_im = turned[:, 0], turned[:, 1]
    product = jnp.stack(
        [jnp.sum(w_re * s_re - w_im * s_im, axis=2), jnp.sum(w_re * s_im + w_im * s_re, axis=2)],
        axis=1,
    )
    product = product.reshape(rep, 2, C, KX, PL).transpose(0, 3, 1, 4, 2)
    product = product.reshape(MX, 2, PL, C)
    wave = to_planes(product)
    spectra = both_samples(spectrum)

    pre, velocity = pl.pallas_call(
        functools.partial(middle_body, scale),
        grid=(xl,),
        out_shape=(
            jax.ShapeDtypeStruct((xl, C, NY, NZ), f32),
            jax.ShapeDtypeStruct((xl, 3, NY, NZ), f32),
        ),
        in_specs=[
            field_spec,
            modes_spec,
            whole(zi.shape),
            whole(yi.shape),
            whole(kw.shape),
            whole(kp.shape),
        ],
        out_specs=(field_spec, vel_spec),
        compiler_params=params,
    )(fields, wave, zi, yi, kw, kp)

    padded = extended(velocity[:, 0].astype(bf16), "gx").astype(f32)
    slope_x = (padded[2:] - padded[:-2]) * 0.5
    divergence = slope_x + central(velocity[:, 1], 1) + central(velocity[:, 2], 2)
    lam = multipliers.astype(f32) / 64.0
    penalty = lam + penalty_weight * divergence
    misfit = velocity - targets.astype(f32)
    loss_sum = (
        jnp.sum(misfit * misfit)
        + jnp.sum(lam * divergence)
        + 0.5 * penalty_weight * jnp.sum(divergence * divergence)
    )
    padded = extended(penalty.astype(bf16), "gx").astype(f32)
    pen_x = (padded[2:] - padded[:-2]) * 0.5
    slopes = jnp.stack([pen_x, central(penalty, 1), central(penalty, 2)], axis=1)
    grad_vel = ((2.0 * misfit - slopes) / rep).astype(bf16)

    wide = C * ROWS
    grad_slab, gw, gq = pl.pallas_call(
        backward_body,
        grid=(xl,),
        out_shape=(
            sums_shape,
            jax.ShapeDtypeStruct((wide, wide), f32),
            jax.ShapeDtypeStruct((wide, 3 * ROWS), f32),
        ),
        in_specs=[
            field_spec,
            field_spec,
            vel_spec,
            whole(ty.shape),
            whole(zt.shape),
            whole(kpt.shape),
        ],
        out_specs=(modes_spec, whole((wide, wide)), whole((wide, 3 * ROWS))),
        scratch_shapes=[pltpu.VMEM((1, C, NY, NZ), bf16)],
        compiler_params=params,
    )(fields, pre, grad_vel, ty, zt, kpt)

    gather = jnp.asarray(np.kron(np.eye(C), np.ones((1, ROWS))).astype(np.float32))
    gather_q = jnp.asarray(np.kron(np.eye(3), np.ones((ROWS, 1))).astype(np.float32))
    mask = jnp.asarray(np.kron(np.ones((C, C)), np.eye(ROWS)).astype(np.float32))
    mask_q = jnp.asarray(np.kron(np.ones((C, 3)), np.eye(ROWS)).astype(np.float32))
    grad_w = jnp.dot(jnp.dot(gather, gw * mask, precision=precise), gather.T, precision=precise)
    grad_q = jnp.dot(jnp.dot(gather, gq * mask_q, precision=precise), gather_q, precision=precise)
    if direct:
        last = jnp.broadcast_to(loss_sum.reshape(1, 1), (C, 1))
        packed = jnp.concatenate([grad_w, grad_q, last], axis=1)
        packed = jnp.pad(packed, ((0, 0), (0, 128 - C - 4)))
        packed = jnp.pad(packed.reshape(-1), (0, EX * 2 * HZ * 128 - C * 128))
        packed = jnp.broadcast_to(packed.reshape(1, EX, 2, HZ, 128), (gx, EX, 2, HZ, 128))
        slab = exchange(lax.dynamic_update_slice(grad_slab, packed, (0, xl, 0, 0, 0)))
        grads = x_modes(slab)
        sums = jnp.sum(slab[:, xl:], axis=0).reshape(-1)
        both = jnp.concatenate(
            [grads.reshape(rep, -1), jnp.broadcast_to(sums[None], (rep, sums.size))], axis=1
        )
        both = lax.all_to_all(both, "rep", split_axis=0, concat_axis=0, tiled=True)
        size = grads.size // rep
        grads = both[:, :size].reshape(rep, MX // rep, 2, PL, C)
        sums = jnp.sum(both[:, size:], axis=0)[: C * 128].reshape(C, 128)
        grad_w, grad_q, loss = sums[:, :C], sums[:, C : C + 3], sums[0, C + 3 : C + 4]
    else:
        grads = both_samples(to_owner(grad_slab))
        packed = jnp.concatenate([grad_w.reshape(-1), grad_q.reshape(-1), loss_sum.reshape(1)])
        packed = lax.psum(packed, ("gx", "rep"))
        grad_w = packed[: C * C].reshape(C, C)
        grad_q = packed[C * C : C * C + 3 * C].reshape(C, 3)
        loss = packed[-1:]
    loss = loss / (rep * NX * NY * NZ)

    g_re, g_im = grads[:, :, 0], grads[:, :, 1]
    across = jnp.stack([jnp.stack([g_re, g_im], 3), jnp.stack([g_im, -g_re], 3)], 1)
    terms = [
        across[b, t][..., None] * spectra[b, :, t][:, :, None, None, :]
        for b in range(rep)
        for t in range(2)
    ]
    grad_r = sum(terms[1:], terms[0])
    return (penalty[None], grad_r, grad_w * scale, grad_q * scale, loss)


def solution(mesh):
    in_specs = (
        P(("grp", "rep"), "gx", None, None, None),
        P(("grp", "rep"), "gx", None, None, None),
        P(("grp", "rep"), "gx", None, None),
        P(),
        P(),
        P("rep", "gx", None, None, None),
    )
    out_specs = (
        P(("grp", "rep"), "gx", None, None),
        P(("grp", "rep"), "gx", None, None, None),
        P("grp", None),
        P("grp", None),
        P("grp"),
    )
    return jax.shard_map(local, mesh=mesh, in_specs=in_specs, out_specs=out_specs, check_vma=False)
```
